512 devices in a mesh: sp: 64 (over x_lo, z, core), hd: 8 (over y, x_hi).
Axes of the slice: x: 4 (x_hi: 2, x_lo: 2; x = x_hi * 2 + x_lo), y: 4, z: 16, core: 2. Of those that a mesh axis runs over, the one named last changes fastest.
Arguments:
- stream: bfloat16 [3, 8, 64, 5120], P(None, 'hd', 'sp'), may hold values from -6 to 6
- queries: bfloat16 [3, 8, 64, 5120], P(None, None, 'sp', 'hd'), may hold values from -40 to 40
- span_k: bfloat16 [3, 8, 64, 5120], P(None, None, 'sp', 'hd'), may hold values from -40 to 40
- span_v: bfloat16 [3, 8, 64, 5120], P(None, None, 'sp', 'hd'), may hold values from -6 to 6
- cache_k: bfloat16 [6144, 5120], P('sp', 'hd'), may hold values from -6 to 6
- cache_v: bfloat16 [6144, 5120], P('sp', 'hd'), may hold values from -6 to 6
- cache_age: int32 [6144], P('sp'), may hold values from 0 to 20, as said below
- history: int32 [1], replicated, may hold values from 1 to 20
- out_weight: bfloat16 [5120, 5120], P('hd', 'sp'), may hold values from -2 to 2
- attn_gate: float32 [5120], replicated, may hold values from 0.5 to 1.5
- head_shift: float32 [5120], replicated, may hold values from -3 to 3
- head_scale: float32 [5120], replicated, may hold values from -1.75 to 1.75
- head_weight: bfloat16 [5120, 64], replicated, may hold values from -0.078125 to 0.078125
- latent_cache: bfloat16 [2, 16, 128, 16], P(None, 'hd', 'sp'), may hold values from -6 to 6
- conv_weight: bfloat16 [432, 384], replicated, may hold values from -0.3125 to 0.3125
- rms_gain: float32 [384], replicated, may hold values from 0.25 to 1.75
Outputs:
- stream_out: bfloat16 [3, 8, 64, 5120], P(None, 'hd', 'sp')
- decoded: bfloat16 [3, 16, 128, 384], P(None, 'hd', 'sp')
The draws below stay inside these ranges and needn't reach their ends.
Inputs may be any that keep to these rules, and one draw needn't show every extreme that they name: `cache_age`: 20 marks an empty cache slot. Among the 96 slots of each index of sp the live ones come first and number at least 24; some index of sp has all its slots live.
All inputs are finite; a program needn't handle non-finite values.
Results may differ from the reference program's by a relative error of at most 0.017.
Values may be sent and summed in bfloat16 or wider, within the bound.
No kernel may reach another device: no remote copies, remote signals or barrier semaphores. Data moves between devices by JAX's collectives and lax.ppermute only.
A program may use at most 64 MiB of HBM per device.

```python
import math
import jax
import jax.numpy as jnp
from jax import lax

D = 5120
HEADS = 40
HDIM = 128
LAT = 16
CHAN = 384
PATCH = 2
FRAMES = 3
MAXH = 20
CSLOT = 96
HT = 8
WT = 64
CROWS = 6144
LH = 16
LW = 128


def drawn_pair(key):
    base_key = jax.random.fold_in(key, 7177)
    key_q, key_k = jax.random.split(base_key, 2)
    full_shape = (FRAMES, HT, WT, D)
    query_base = 1.4 * jax.random.truncated_normal(key_q, -4.0, 4.0, full_shape, jnp.float32)
    key_base = jax.random.truncated_normal(key_k, -4.0, 4.0, full_shape, jnp.float32)
    return (query_base, key_base)


def draw_queries(key, part):
    return drawn_pair(key)[0].astype(jnp.bfloat16)


def draw_span_k(key, part):
    return drawn_pair(key)[1].astype(jnp.bfloat16)


def draw_cache_age(key, part):
    key_live, key_full, key_age = jax.random.split(jax.random.fold_in(key, 3301), 3)
    groups = CROWS // CSLOT
    live_count = jax.random.randint(key_live, (groups,), CSLOT // 4, CSLOT + 1)
    full_device = jax.random.randint(key_full, (), 0, groups)
    live_count = jnp.where(jnp.arange(groups) == full_device, CSLOT, live_count)
    age_draw = jax.random.randint(key_age, (CROWS,), 0, MAXH)
    slot_pos = jnp.arange(CROWS) % CSLOT
    owner_row = jnp.arange(CROWS) // CSLOT
    return jnp.where(slot_pos < live_count[owner_row], age_draw, MAXH).astype(jnp.int32)


def levels(rng, dims, cuts, smallest, high):
    level = 1.0
    for axis_at, shards_of in cuts:
        steps = jax.random.uniform(jax.random.fold_in(jax.random.fold_in(rng, 6), axis_at), (shards_of,), jnp.float32, smallest / len(cuts), high / len(cuts))
        level = level * jnp.repeat(jnp.exp(steps), dims[axis_at] // shards_of).reshape((-1,) + (1,) * (len(dims) - 1 - axis_at))
    return level


def scatter_about(rng, shape, scale, reach, cuts=(), dtype=jnp.bfloat16):
    factor_of = levels(rng, shape, cuts, -0.22, 0.18) if cuts else 1.0
    drawn = jax.random.normal(rng, shape, jnp.float32) * scale * factor_of
    return jnp.minimum(jnp.maximum(drawn, -reach), reach).astype(dtype)


def setup_inputs(seed: int = 0) -> dict:
    key_list = jax.random.split(jax.random.key(seed), 17)
    stream = scatter_about(key_list[0], (FRAMES, HT, WT, D), 1.0, 6.0, ((1, 8), (2, 64)))
    queries = draw_queries(jax.random.fold_in(key_list[16], 71), 0)
    span_k = draw_span_k(jax.random.fold_in(key_list[16], 71), 0)
    span_v = scatter_about(key_list[3], (FRAMES, HT, WT, D), 1.0, 6.0, ((2, 64), (3, 8)))
    cache_k = scatter_about(key_list[4], (CROWS, D), 1.0, 6.0, ((0, 64), (1, 8)))
    cache_v = scatter_about(key_list[5], (CROWS, D), 1.0, 6.0, ((0, 64), (1, 8)))
    cache_age = draw_cache_age(jax.random.fold_in(key_list[16], 71), 0)
    history = jax.random.randint(key_list[7], (1,), 1, MAXH + 1).astype(jnp.int32)
    out_weight = scatter_about(key_list[8], (D, D), (max(HDIM // 16, 1)) ** -0.5, 2.0, ((0, 8), (1, 64)))
    attn_gate = jnp.clip(jax.random.uniform(key_list[9], (D,), jnp.float32, 0.5, 1.5), 0.5, 1.5)
    head_shift = scatter_about(key_list[10], (D,), 0.5, 3.0, (), jnp.float32)
    head_scale = scatter_about(key_list[11], (D,), 0.3, 1.75, (), jnp.float32)
    head_weight = scatter_about(key_list[12], (D, PATCH * PATCH * LAT), D ** -0.5, 0.078125)
    latent_cache = scatter_about(key_list[13], (2, LH, LW, LAT), 1.0, 6.0, ((1, 8), (2, 64)))
    conv_weight = scatter_about(key_list[14], (27 * LAT, CHAN), (27 * LAT) ** -0.5, 0.3125)
    rms_gain = jnp.clip(1.0 + 0.15 * jax.random.normal(key_list[15], (CHAN,), jnp.float32), 0.25, 1.75)
    return dict(stream=stream, queries=queries, span_k=span_k, span_v=span_v, cache_k=cache_k, cache_v=cache_v, cache_age=cache_age, history=history, out_weight=out_weight, attn_gate=attn_gate, head_shift=head_shift, head_scale=head_scale, head_weight=head_weight, latent_cache=latent_cache, conv_weight=conv_weight, rms_gain=rms_gain)


def causal_conv(padded, frames, height, breadth, conv_weight, rms_gain):
    tap_list = []
    for step_t in range(3):
        for step_i in range(3):
            for step_j in range(3):
                tap_list.append(padded[step_t:step_t + frames, step_i:step_i + height, step_j:step_j + breadth, :])
    patches = jnp.concatenate(tap_list, axis=-1)
    conv_out = jnp.dot(patches.reshape(-1, patches.shape[-1]), conv_weight, preferred_element_type=jnp.float32)
    mean_square = lax.optimization_barrier(jnp.mean(conv_out * conv_out, axis=-1, keepdims=True))
    scaled = conv_out * lax.rsqrt(mean_square + 1e-06) * rms_gain
    return jax.nn.silu(scaled).astype(jnp.bfloat16).reshape(frames, height, breadth, -1)

def reference(stream, queries, span_k, span_v, cache_k, cache_v, cache_age, history, out_weight, attn_gate, head_shift, head_scale, head_weight, latent_cache, conv_weight, rms_gain):
    query_count = FRAMES * HT * WT
    factor = 1.0 / math.sqrt(HDIM)
    query_all = queries.reshape(query_count, HEADS, HDIM).astype(jnp.float32)
    group_ck = cache_k.reshape(WT, CSLOT, D)
    group_cv = cache_v.reshape(WT, CSLOT, D)
    group_age = cache_age.reshape(WT, CSLOT)
    group_nk = jnp.transpose(span_k, (2, 0, 1, 3)).reshape(WT, FRAMES * HT, D)
    group_nv = jnp.transpose(span_v, (2, 0, 1, 3)).reshape(WT, FRAMES * HT, D)

    def group_step(carry, group):
        run_top, run_total, run_out = carry
        cache_keys, cache_vals, slot_age, new_keys, new_vals = group
        key_all = jnp.concatenate([cache_keys, new_keys], axis=0).reshape(-1, HEADS, HDIM).astype(jnp.float32)
        val_all = jnp.concatenate([cache_vals, new_vals], axis=0).reshape(-1, HEADS, HDIM).astype(jnp.float32)
        is_valid = jnp.concatenate([slot_age < history[0], jnp.ones((FRAMES * HT,), jnp.bool_)])
        scores = jnp.einsum('qhd,khd->hqk', query_all, key_all) * factor
        scores = jnp.where(is_valid[None, None, :], scores, -1e+30)
        group_max = lax.optimization_barrier(jnp.max(scores, axis=2))
        rounded = lax.optimization_barrier(jnp.exp(scores - group_max[:, :, None]).astype(jnp.bfloat16))
        weights = rounded.astype(jnp.float32)
        group_total = lax.optimization_barrier(jnp.sum(weights, axis=2))
        group_out = jnp.einsum('hqk,khd->hqd', weights, val_all)
        new_top = jnp.maximum(run_top, group_max)
        old_w = jnp.exp(run_top - new_top)
        new_w = jnp.exp(group_max - new_top)
        return ((new_top, run_total * old_w + group_total * new_w, run_out * old_w[:, :, None] + group_out * new_w[:, :, None]), None)
    start_carry = (jnp.full((HEADS, query_count), -1e+30, jnp.float32), jnp.zeros((HEADS, query_count), jnp.float32), jnp.zeros((HEADS, query_count, HDIM), jnp.float32))
    final_carry, _ = lax.scan(group_step, start_carry, (group_ck, group_cv, group_age, group_nk, group_nv))
    attended_f = final_carry[2] / final_carry[1][:, :, None]
    attended = jnp.transpose(attended_f, (1, 0, 2)).reshape(query_count, D).astype(jnp.bfloat16)
    projected = jnp.dot(attended, out_weight, preferred_element_type=jnp.float32).reshape(FRAMES, HT, WT, D)
    stream_out = (stream.astype(jnp.float32) + attn_gate * projected).astype(jnp.bfloat16)
    mixed_f = stream_out.astype(jnp.float32)
    centre_mean = lax.optimization_barrier(jnp.mean(mixed_f, axis=-1, keepdims=True))
    centred = mixed_f - centre_mean
    variance = lax.optimization_barrier(jnp.mean(centred * centred, axis=-1, keepdims=True))
    normed = (centred * lax.rsqrt(variance + 1e-06) * (1.0 + head_scale) + head_shift).astype(jnp.bfloat16)
    patch_values = jnp.dot(normed.reshape(-1, D), head_weight, preferred_element_type=jnp.float32).astype(jnp.bfloat16)
    patch_values = patch_values.reshape(FRAMES, HT, WT, PATCH, PATCH, LAT)
    latent = jnp.transpose(patch_values, (0, 1, 3, 2, 4, 5)).reshape(FRAMES, HT * PATCH, WT * PATCH, LAT)
    sequence = jnp.concatenate([latent_cache, latent], axis=0)
    padded = jnp.pad(sequence, ((0, 0), (1, 1), (1, 1), (0, 0)))
    decoded = causal_conv(padded, FRAMES, HT * PATCH, WT * PATCH, conv_weight, rms_gain)
    return (stream_out, decoded)
```

```python
import functools
import math

import jax
import jax.numpy as jnp
from jax import lax
from jax.experimental import pallas as pl
from jax.experimental.pallas import tpu as pltpu
from jax.sharding import Mesh
from jax.sharding import PartitionSpec as P

HDIM = 128
LAT = 16
PATCH = 2
KEYS = 128
NEG = -1e30


BF = jnp.bfloat16
F32 = jnp.float32


def full_call(body, out_shape, scratch=()):
    return pl.pallas_call(
        body,
        out_shape=out_shape,
        scratch_shapes=list(scratch),
        compiler_params=pltpu.CompilerParams(vmem_limit_bytes=48 * 1024 * 1024),
    )


def two_parts(value):
    high = value.astype(BF).astype(F32)
    low = (value - high).astype(BF).astype(F32)
    return high, low


def block_body(age_ref, history_ref, cache_k_ref, span_k_ref, cache_v_ref, span_v_ref, out_ref):
    slots, width = cache_k_ref.shape
    tokens = span_k_ref.shape[0]
    live = slots + tokens
    out_ref[0:slots] = cache_k_ref[...]
    out_ref[slots:live] = span_k_ref[...]
    out_ref[KEYS : KEYS + slots] = cache_v_ref[...]
    out_ref[KEYS + slots : KEYS + live] = span_v_ref[...]
    out_ref[KEYS + live :] = jnp.zeros((KEYS - live, width), BF)
    valid = jnp.where(age_ref[...] < history_ref[0], 1.0, 0.0)
    flags = jnp.concatenate(
        [valid, jnp.ones((1, tokens), F32), jnp.zeros((1, width - live), F32)], axis=1
    )
    out_ref[live:KEYS] = jnp.broadcast_to(flags, (KEYS - live, width)).astype(BF)


def attend_body(q_ref, near_ref, far_ref, out_ref, *, heads, tokens, step):
    places = q_ref.shape[0]
    groups = tokens // 8
    rate = math.log2(math.e) / math.sqrt(HDIM)
    rows = step * tokens
    row = lax.broadcasted_iota(jnp.int32, (rows, 128), 0)
    lane = lax.broadcasted_iota(jnp.int32, (rows, 128), 1)
    group_lane = lane - heads * ((row % tokens) // 8)
    key_row = lax.broadcasted_iota(jnp.int32, (KEYS, KEYS), 0)
    key_lane = lax.broadcasted_iota(jnp.int32, (KEYS, KEYS), 1)
    first = key_lane == 0
    query_tail = jnp.where(lane == 0, 1.0, 0.0).astype(BF)
    value_tail = jnp.where(first, 1.0, 0.0).astype(BF)
    value_tail = jnp.concatenate([value_tail, value_tail], axis=0)
    key_tails = []
    for ref in (near_ref, far_ref):
        tails = []
        for d in range(2):
            flags = ref[d, KEYS - 8 : KEYS, 0:KEYS].astype(F32)[0:1]
            valid = jnp.sum(jnp.where(key_row == key_lane, flags, 0.0), axis=1, keepdims=True)
            tails.append(jnp.where(first, (1.0 - valid) * NEG, 0.0).astype(BF))
        key_tails.append(jnp.concatenate(tails, axis=0))
    for head in range(heads):
        cols = slice(head * HDIM, (head + 1) * HDIM)
        keys = [
            jnp.concatenate([ref[:, 0:KEYS, cols].reshape(2 * KEYS, HDIM), tail], axis=1)
            for ref, tail in zip((near_ref, far_ref), key_tails)
        ]
        vals = [
            jnp.concatenate([ref[:, KEYS : 2 * KEYS, cols].reshape(2 * KEYS, HDIM), value_tail], axis=1)
            for ref in (near_ref, far_ref)
        ]
        for start in range(0, places, step):
            query = q_ref[start : start + step, :, cols].reshape(rows, HDIM)
            query = jnp.concatenate([query, query_tail], axis=1)
            scores = [
                lax.dot_general(query, k, (((1,), (1,)), ((), ())), preferred_element_type=F32) for k in keys
            ]
            top = jnp.max(jnp.maximum(scores[0], scores[1]), axis=1, keepdims=True)
            top_high, top_low = two_parts(top)
            top = top_high + top_low
            out = sum(
                jnp.dot(jnp.exp2((s - top) * rate).astype(BF), v, preferred_element_type=F32)
                for s, v in zip(scores, vals)
            )
            sum_high, sum_low = two_parts(out[:, HDIM : HDIM + 1])
            at = slice(head * tokens, (head + 1) * tokens)
            out_ref[start : start + step, at, :] = out[:, 0:HDIM].reshape(step, tokens, HDIM).astype(BF)
            stats = jnp.zeros((rows, 128), F32)
            for k, part in enumerate((top_high, top_low, sum_high, sum_low)):
                stats = jnp.where(group_lane == 32 * k + head, part, stats)
            folded = stats.reshape(step, groups, 8, 128).sum(axis=1)
            at = slice(heads * tokens, heads * tokens + 8)
            if head:
                folded = folded + out_ref[start : start + step, at, :].astype(F32)
            out_ref[start : start + step, at, :] = folded.astype(BF)


def merge_body(in_ref, out_ref, *, heads, tokens):
    groups = tokens // 8
    stats = in_ref[:, heads * tokens :, :].astype(F32)
    top = stats + pltpu.roll(stats, 96, 2)
    total = pltpu.roll(stats, 64, 2) + pltpu.roll(stats, 32, 2)
    peak = jnp.max(top, axis=0, keepdims=True)
    factor = jnp.exp((top - peak) * (1.0 / math.sqrt(HDIM)))
    lane = lax.broadcasted_iota(jnp.int32, (1, 8, 128), 2)
    total = jnp.where(lane < groups * heads, total, 1.0)
    factor = jnp.where(lane < groups * heads, factor, 1.0)
    share = factor / jnp.sum(factor * total, axis=0, keepdims=True)
    for head in range(heads):
        for group in range(groups):
            at = head * tokens + group * 8
            weight = share[:, :, group * heads + head : group * heads + head + 1]
            part = in_ref[:, at : at + 8, :].astype(F32) * weight
            out_ref[group * 8 : group * 8 + 8, head * HDIM : (head + 1) * HDIM] = jnp.sum(
                part, axis=0
            ).astype(BF)


def project_body(att_ref, weight_ref, out_ref, *, frames, token_rows):
    count = att_ref.shape[0]
    tokens = frames * token_rows
    i = lax.broadcasted_iota(jnp.int32, (count, count), 0)
    j = lax.broadcasted_iota(jnp.int32, (count, count), 1)
    source = (i // tokens) * tokens + (i % frames) * token_rows + (i % tokens) // frames
    order = jnp.where(j == source, 1.0, 0.0).astype(BF)
    att = jnp.dot(order, att_ref[...], preferred_element_type=F32).astype(BF)
    out = lax.dot_general(
        att, weight_ref[...], (((1,), (1,)), ((), ())), preferred_element_type=F32
    ).astype(BF)
    for n in range(count // frames):
        out_ref[n] = out[n * frames : (n + 1) * frames]


def head_body(
    in_ref, stream_ref, gate_ref, shift_ref, scale_ref, weight_ref, stream_out_ref, patch_ref, sum_ref, *, parts, pairs, places
):
    blocks = 2 * pairs
    per = in_ref.shape[0] // blocks
    width = in_ref.shape[2] // places
    for block in range(blocks):
        total = in_ref[block * per].astype(F32)
        for k in range(1, per):
            total = total + in_ref[block * per + k].astype(F32)
        outer, inner = block // 2, block % 2
        for place in range(places):
            at = ((outer * places + place) * 2 + inner) * width
            sum_ref[:, at : at + width] = total[:, place * width : (place + 1) * width]
    mixed = (stream_ref[...].astype(F32) + gate_ref[...] * sum_ref[...]).astype(BF)
    stream_out_ref[...] = mixed
    mixed = mixed.astype(F32)
    mean = jnp.mean(mixed, axis=-1, keepdims=True)
    centred = mixed - mean
    variance = jnp.mean(centred * centred, axis=-1, keepdims=True)
    normed = (centred * lax.rsqrt(variance + 1e-06) * (1.0 + scale_ref[...]) + shift_ref[...]).astype(BF)
    patch_ref[...] = lax.dot_general(
        normed, weight_ref[...], (((1,), (1,)), ((), ())), preferred_element_type=F32
    ).astype(BF)


def conv_body(odd_ref, above_ref, mid_ref, below_ref, weight_ref, gain_ref, out_ref, patch_ref, *, frames):
    def placed(first, own, second, odd):
        first, second = first.astype(F32), second.astype(F32)
        return jnp.where(odd, first, second), own.astype(F32), jnp.where(odd, second, first)

    odd_col, odd_row = odd_ref[0] == 1, odd_ref[1] == 1
    rows = [placed(ref[0], ref[1], ref[2], odd_col) for ref in (above_ref, mid_ref, below_ref)]
    by_col = [placed(rows[0][c], rows[1][c], rows[2][c], odd_row) for c in range(3)]
    for a in range(PATCH):
        for b in range(PATCH):
            pieces = []
            for u in range(3):
                for v in range(3):
                    for w in range(3):
                        i, j = a + v - 1, b + w - 1
                        block = by_col[j // 2 + 1][i // 2 + 1]
                        at = ((i % 2) * 2 + (j % 2)) * LAT
                        pieces.append(block[u : u + frames, at : at + LAT])
            patch_ref[(a * 2 + b) * 8 : (a * 2 + b) * 8 + frames, :] = jnp.concatenate(pieces, axis=1)
    patches = patch_ref[...].astype(BF)
    conv = jnp.dot(patches, weight_ref[...], preferred_element_type=F32)
    square = jnp.mean(conv * conv, axis=-1, keepdims=True)
    scaled = conv * lax.rsqrt(square + 1e-06) * gain_ref[...]
    silu = (scaled / (1.0 + jnp.exp(-scaled))).astype(BF)
    for f in range(frames):
        for a in range(PATCH):
            for b in range(PATCH):
                at = (a * 2 + b) * 8 + f
                out_ref[f, a, b : b + 1, :] = silu[at : at + 1, :]


COL = ("xl", "z", "core")
ROW = ("y", "xh")


def swaps(cells, axes):
    count = lax.axis_size(axes)
    out = []
    for start in (0, 1):
        pairs = [(i, i + 1) for i in range(start, count - 1, 2)]
        out.append(lax.ppermute(cells, axes, pairs + [(j, i) for i, j in pairs]))
    return out


def local(
    stream,
    queries,
    span_k,
    span_v,
    cache_k,
    cache_v,
    cache_age,
    history,
    out_weight,
    attn_gate,
    head_shift,
    head_scale,
    head_weight,
    latent_cache,
    conv_weight,
    rms_gain,
):
    frames, token_rows, _, width = queries.shape
    tokens = frames * token_rows
    heads = width // HDIM
    places = lax.axis_size("z")
    features = stream.shape[-1]

    weights = lax.all_gather(out_weight.T, "z", axis=0, tiled=True)

    own = pl.pallas_call(
        block_body,
        out_shape=jax.ShapeDtypeStruct((2 * KEYS, width), BF),
        in_specs=[pl.BlockSpec(), pl.BlockSpec(memory_space=pltpu.SMEM)] + [pl.BlockSpec()] * 4,
    )(
        cache_age[None, :],
        history,
        cache_k,
        span_k.reshape(tokens, width),
        cache_v,
        span_v.reshape(tokens, width),
    )
    near = lax.all_gather(own, "core", axis=0)
    far = lax.ppermute(near, "xl", [(0, 1), (1, 0)])
    gathered = lax.all_gather(queries.reshape(tokens, width), "z", axis=0)
    partial = full_call(
        functools.partial(attend_body, heads=heads, tokens=tokens, step=4),
        jax.ShapeDtypeStruct((places, heads * tokens + 8, HDIM), BF),
    )(gathered, near, far)
    partial = lax.all_to_all(partial, "z", 0, 0, tiled=True)
    attended = full_call(
        functools.partial(merge_body, heads=heads, tokens=tokens),
        jax.ShapeDtypeStruct((tokens, width), BF),
    )(partial)
    attended, weights = lax.optimization_barrier((attended, weights))
    group = lax.all_gather(attended, ("xl", "core"), axis=0, tiled=True)
    terms = full_call(
        functools.partial(project_body, frames=frames, token_rows=token_rows),
        jax.ShapeDtypeStruct((4 * token_rows, frames, weights.shape[0]), BF),
    )(group, weights)
    terms = lax.all_to_all(terms, ("xl", "core") + ROW, 0, 0, tiled=True)
    stream_out, patch = full_call(
        functools.partial(head_body, parts=4, pairs=2, places=places),
        (
            jax.ShapeDtypeStruct((frames, features), BF),
            jax.ShapeDtypeStruct((frames, head_weight.shape[1]), BF),
        ),
        [pltpu.VMEM((frames, features), F32)],
    )(
        terms,
        stream.reshape(frames, features),
        attn_gate[None, :],
        head_shift[None, :],
        head_scale[None, :],
        head_weight.T,
    )
    cells = jnp.concatenate([latent_cache.reshape(2, -1), patch], axis=0)
    first, second = swaps(cells, COL)
    across = jnp.stack([first, cells, second])
    first, second = swaps(across, ROW)
    odd = jnp.stack([lax.axis_index("core"), lax.axis_index("xh")]).astype(jnp.int32)
    decoded = pl.pallas_call(
        functools.partial(conv_body, frames=frames),
        out_shape=jax.ShapeDtypeStruct((frames, PATCH, PATCH, conv_weight.shape[1]), BF),
        in_specs=[pl.BlockSpec(memory_space=pltpu.SMEM)] + [pl.BlockSpec()] * 5,
        scratch_shapes=[pltpu.VMEM((32, conv_weight.shape[0]), F32)],
    )(odd, first, across, second, conv_weight, rms_gain[None, :])
    return stream_out.reshape(stream.shape), decoded


def solution(mesh):
    fine = Mesh(mesh.devices.reshape(2, 16, 2, 4, 2), COL + ROW)
    placed = (
        P(None, ROW, COL, None),
        P(None, None, COL, ROW),
        P(None, None, COL, ROW),
        P(None, None, COL, ROW),
        P(COL, ROW),
        P(COL, ROW),
        P(COL),
        P(),
        P(ROW, COL),
        P(),
        P(),
        P(),
        P(),
        P(None, ROW, COL, None),
        P(),
        P(),
    )
    return jax.shard_map(
        local,
        mesh=fine,
        in_specs=placed,
        out_specs=(P(None, ROW, COL, None), P(None, ROW, COL, None)),
        check_vma=False,
    )
```

```python
import functools
import math

import jax
import jax.numpy as jnp
from jax import lax
from jax.experimental import pallas as pl
from jax.experimental.pallas import tpu as pltpu
from jax.sharding import Mesh
from jax.sharding import PartitionSpec as P

HDIM = 128
LAT = 16
PATCH = 2
KEYS = 128
NEG = -1e30


BF = jnp.bfloat16
F32 = jnp.float32


def full_call(body, out_shape, scratch=(), limit=24 * 1024 * 1024, **specs):
    return pl.pallas_call(
        body,
        out_shape=out_shape,
        scratch_shapes=list(scratch),
        compiler_params=pltpu.CompilerParams(vmem_limit_bytes=limit),
        **specs,
    )


def two_parts(value):
    high = value.astype(BF).astype(F32)
    low = (value - high).astype(BF).astype(F32)
    return high, low


def block_body(age_ref, history_ref, cache_k_ref, span_k_ref, cache_v_ref, span_v_ref, out_ref):
    slots, width = cache_k_ref.shape
    tokens = span_k_ref.shape[0]
    live = slots + tokens
    out_ref[0:slots] = cache_k_ref[...]
    out_ref[slots:live] = span_k_ref[...]
    out_ref[KEYS : KEYS + slots] = cache_v_ref[...]
    out_ref[KEYS + slots : KEYS + live] = span_v_ref[...]
    out_ref[KEYS + live :] = jnp.zeros((KEYS - live, width), BF)
    valid = jnp.where(age_ref[...] < history_ref[0], 1.0, 0.0)
    flags = jnp.concatenate(
        [valid, jnp.ones((1, tokens), F32), jnp.zeros((1, width - live), F32)], axis=1
    )
    out_ref[live:KEYS] = jnp.broadcast_to(flags, (KEYS - live, width)).astype(BF)


def attend_body(q_ref, near_ref, far_ref, out_ref, *, heads, tokens, step):
    places = q_ref.shape[0]
    groups = tokens // 8
    rate = math.log2(math.e) / math.sqrt(HDIM)
    rows = step * tokens
    row = lax.broadcasted_iota(jnp.int32, (rows, 128), 0)
    lane = lax.broadcasted_iota(jnp.int32, (rows, 128), 1)
    group_lane = lane - heads * ((row % tokens) // 8)
    lane_key = lax.broadcasted_iota(jnp.int32, (2 * KEYS, HDIM), 1)
    value_tail = jnp.where(lane_key == 0, 1.0, 0.0).astype(BF)
    masks = []
    for ref in (near_ref, far_ref):
        flags = [ref[d, KEYS - 8 : KEYS, 0:KEYS].astype(F32)[0:1] for d in range(2)]
        masks.append((1.0 - jnp.concatenate(flags, axis=1)) * NEG)
    for head in range(heads):
        cols = slice(head * HDIM, (head + 1) * HDIM)
        keys = [ref[:, 0:KEYS, cols].reshape(2 * KEYS, HDIM) for ref in (near_ref, far_ref)]
        vals = [
            jnp.concatenate([ref[:, KEYS : 2 * KEYS, cols].reshape(2 * KEYS, HDIM), value_tail], axis=1)
            for ref in (near_ref, far_ref)
        ]
        for start in range(0, places, step):
            query = q_ref[start : start + step, :, cols].reshape(rows, HDIM)
            scores = [
                lax.dot_general(query, k, (((1,), (1,)), ((), ())), preferred_element_type=F32) + mask
                for k, mask in zip(keys, masks)
            ]
            top = jnp.max(jnp.maximum(scores[0], scores[1]), axis=1, keepdims=True)
            top_high, top_low = two_parts(top)
            top = top_high + top_low
            out = sum(
                jnp.dot(jnp.exp2((s - top) * rate).astype(BF), v, preferred_element_type=F32)
                for s, v in zip(scores, vals)
            )
            sum_high, sum_low = two_parts(out[:, HDIM : HDIM + 1])
            at = slice(head * tokens, (head + 1) * tokens)
            out_ref[start : start + step, at, :] = out[:, 0:HDIM].reshape(step, tokens, HDIM).astype(BF)
            stats = jnp.zeros((rows, 128), F32)
            for k, part in enumerate((top_high, top_low, sum_high, sum_low)):
                stats = jnp.where(group_lane == 32 * k + head, part, stats)
            folded = stats.reshape(step, groups, 8, 128).sum(axis=1)
            at = slice(heads * tokens, heads * tokens + 8)
            if head:
                folded = folded + out_ref[start : start + step, at, :].astype(F32)
            out_ref[start : start + step, at, :] = folded.astype(BF)


def merge_body(in_ref, out_ref, *, heads, tokens):
    groups = tokens // 8
    stats = in_ref[:, heads * tokens :, :].astype(F32)
    top = stats + pltpu.roll(stats, 96, 2)
    total = pltpu.roll(stats, 64, 2) + pltpu.roll(stats, 32, 2)
    peak = jnp.max(top, axis=0, keepdims=True)
    factor = jnp.exp((top - peak) * (1.0 / math.sqrt(HDIM)))
    lane = lax.broadcasted_iota(jnp.int32, (1, 8, 128), 2)
    total = jnp.where(lane < groups * heads, total, 1.0)
    factor = jnp.where(lane < groups * heads, factor, 1.0)
    share = factor / jnp.sum(factor * total, axis=0, keepdims=True)
    for head in range(heads):
        for group in range(groups):
            at = head * tokens + group * 8
            weight = share[:, :, group * heads + head : group * heads + head + 1]
            part = in_ref[:, at : at + 8, :].astype(F32) * weight
            out_ref[group * 8 : group * 8 + 8, head * HDIM : (head + 1) * HDIM] = jnp.sum(
                part, axis=0
            ).astype(BF)


def project_body(att_ref, weight_ref, out_ref, *, frames, token_rows):
    count = att_ref.shape[0]
    tokens = frames * token_rows
    i = lax.broadcasted_iota(jnp.int32, (count, count), 0)
    j = lax.broadcasted_iota(jnp.int32, (count, count), 1)
    source = (i // tokens) * tokens + (i % frames) * token_rows + (i % tokens) // frames
    order = jnp.where(j == source, 1.0, 0.0).astype(BF)
    att = jnp.dot(order, att_ref[...], preferred_element_type=F32).astype(BF)
    out = lax.dot_general(
        att, weight_ref[...], (((1,), (1,)), ((), ())), preferred_element_type=F32
    ).astype(BF)
    for n in range(count // frames):
        out_ref[n] = out[n * frames : (n + 1) * frames]


def head_body(
    in_ref, stream_ref, gate_ref, shift_ref, scale_ref, weight_ref, stream_out_ref, patch_ref, sum_ref, *, parts, pairs, places
):
    blocks = 2 * pairs
    per = in_ref.shape[0] // blocks
    width = in_ref.shape[2] // places
    for block in range(blocks):
        total = in_ref[block * per].astype(F32)
        for k in range(1, per):
            total = total + in_ref[block * per + k].astype(F32)
        outer, inner = block // 2, block % 2
        for place in range(places):
            at = ((outer * places + place) * 2 + inner) * width
            sum_ref[:, at : at + width] = total[:, place * width : (place + 1) * width]
    mixed = (stream_ref[...].astype(F32) + gate_ref[...] * sum_ref[...]).astype(BF)
    stream_out_ref[...] = mixed
    mixed = mixed.astype(F32)
    mean = jnp.mean(mixed, axis=-1, keepdims=True)
    centred = mixed - mean
    variance = jnp.mean(centred * centred, axis=-1, keepdims=True)
    normed = (centred * lax.rsqrt(variance + 1e-06) * (1.0 + scale_ref[...]) + shift_ref[...]).astype(BF)
    patch_ref[...] = lax.dot_general(
        normed, weight_ref[...], (((1,), (1,)), ((), ())), preferred_element_type=F32
    ).astype(BF)


def conv_body(above_ref, mid_ref, below_ref, weight_ref, gain_ref, out_ref, patch_ref, *, frames):
    def placed(first, own, second, odd):
        first, second = first.astype(F32), second.astype(F32)
        return jnp.where(odd, first, second), own.astype(F32), jnp.where(odd, second, first)

    odd_col, odd_row = lax.axis_index("core") == 1, lax.axis_index("xh") == 1
    rows = [placed(ref[0], ref[1], ref[2], odd_col) for ref in (above_ref, mid_ref, below_ref)]
    by_col = [placed(rows[0][c], rows[1][c], rows[2][c], odd_row) for c in range(3)]
    for a in range(PATCH):
        for b in range(PATCH):
            pieces = []
            for u in range(3):
                for v in range(3):
                    for w in range(3):
                        i, j = a + v - 1, b + w - 1
                        block = by_col[j // 2 + 1][i // 2 + 1]
                        at = ((i % 2) * 2 + (j % 2)) * LAT
                        pieces.append(block[u : u + frames, at : at + LAT])
            patch_ref[(a * 2 + b) * 8 : (a * 2 + b) * 8 + frames, :] = jnp.concatenate(pieces, axis=1)
    patches = patch_ref[...].astype(BF)
    conv = jnp.dot(patches, weight_ref[...], preferred_element_type=F32)
    square = jnp.mean(conv * conv, axis=-1, keepdims=True)
    scaled = conv * lax.rsqrt(square + 1e-06) * gain_ref[...]
    silu = (scaled / (1.0 + jnp.exp(-scaled))).astype(BF)
    for f in range(frames):
        for a in range(PATCH):
            for b in range(PATCH):
                at = (a * 2 + b) * 8 + f
                out_ref[f, a, b : b + 1, :] = silu[at : at + 1, :]


COL = ("xl", "z", "core")
ROW = ("y", "xh")


def swaps(cells, axes):
    count = lax.axis_size(axes)
    out = []
    for start in (0, 1):
        pairs = [(i, i + 1) for i in range(start, count - 1, 2)]
        out.append(lax.ppermute(cells, axes, pairs + [(j, i) for i, j in pairs]))
    return out


def local(
    stream,
    queries,
    span_k,
    span_v,
    cache_k,
    cache_v,
    cache_age,
    history,
    out_weight,
    attn_gate,
    head_shift,
    head_scale,
    head_weight,
    latent_cache,
    conv_weight,
    rms_gain,
):
    frames, token_rows, _, width = queries.shape
    tokens = frames * token_rows
    heads = width // HDIM
    places = lax.axis_size("z")
    features = stream.shape[-1]

    weights = lax.all_gather(out_weight.T, "z", axis=0, tiled=True)

    own = full_call(
        block_body,
        jax.ShapeDtypeStruct((2 * KEYS, width), BF),
        limit=None,
        in_specs=[pl.BlockSpec(), pl.BlockSpec(memory_space=pltpu.SMEM)] + [pl.BlockSpec()] * 4,
    )(
        cache_age[None, :],
        history,
        cache_k,
        span_k.reshape(tokens, width),
        cache_v,
        span_v.reshape(tokens, width),
    )
    near = lax.all_gather(own, "core", axis=0)
    far = lax.ppermute(near, "xl", [(0, 1), (1, 0)])
    gathered = lax.all_gather(queries.reshape(tokens, width), "z", axis=0)
    partial = full_call(
        functools.partial(attend_body, heads=heads, tokens=tokens, step=8),
        jax.ShapeDtypeStruct((places, heads * tokens + 8, HDIM), BF),
    )(gathered, near, far)
    partial = lax.all_to_all(partial, "z", 0, 0, tiled=True)
    attended = full_call(
        functools.partial(merge_body, heads=heads, tokens=tokens),
        jax.ShapeDtypeStruct((tokens, width), BF),
    )(partial)
    group = lax.all_gather(attended, ("xl", "core"), axis=0, tiled=True)
    terms = full_call(
        functools.partial(project_body, frames=frames, token_rows=token_rows),
        jax.ShapeDtypeStruct((4 * token_rows, frames, weights.shape[0]), BF),
    )(group, weights)
    terms = lax.all_to_all(terms, ("xl", "core") + ROW, 0, 0, tiled=True)
    stream_out, patch = full_call(
        functools.partial(head_body, parts=4, pairs=2, places=places),
        (
            jax.ShapeDtypeStruct((frames, features), BF),
            jax.ShapeDtypeStruct((frames, head_weight.shape[1]), BF),
        ),
        [pltpu.VMEM((frames, features), F32)],
    )(
        terms,
        stream.reshape(frames, features),
        attn_gate[None, :],
        head_shift[None, :],
        head_scale[None, :],
        head_weight.T,
    )
    cells = jnp.concatenate([latent_cache.reshape(2, -1), patch], axis=0)
    first, second = swaps(cells, COL)
    across = jnp.stack([first, cells, second])
    first, second = swaps(across, ROW)
    decoded = full_call(
        functools.partial(conv_body, frames=frames),
        jax.ShapeDtypeStruct((frames, PATCH, PATCH, conv_weight.shape[1]), BF),
        [pltpu.VMEM((32, conv_weight.shape[0]), F32)],
    )(first, across, second, conv_weight, rms_gain[None, :])
    return stream_out.reshape(stream.shape), decoded


def solution(mesh):
    fine = Mesh(mesh.devices.reshape(2, 16, 2, 4, 2), COL + ROW)
    placed = (
        P(None, ROW, COL, None),
        P(None, None, COL, ROW),
        P(None, None, COL, ROW),
        P(None, None, COL, ROW),
        P(COL, ROW),
        P(COL, ROW),
        P(COL),
        P(),
        P(ROW, COL),
        P(),
        P(),
        P(),
        P(),
        P(None, ROW, COL, None),
        P(),
        P(),
    )
    return jax.shard_map(
        local,
        mesh=fine,
        in_specs=placed,
        out_specs=(P(None, ROW, COL, None), P(None, ROW, COL, None)),
        check_vma=False,
    )
```

```python
import functools
import math

import jax
import jax.numpy as jnp
from jax import lax
from jax.experimental import pallas as pl
from jax.experimental.pallas import tpu as pltpu
from jax.sharding import Mesh
from jax.sharding import PartitionSpec as P

HDIM = 128
LAT = 16
PATCH = 2
KEYS = 128
NEG = -1e30


BF = jnp.bfloat16
F32 = jnp.float32


def full_call(body, out_shape, scratch=(), limit=24 * 1024 * 1024, **specs):
    return pl.pallas_call(
        body,
        out_shape=out_shape,
        scratch_shapes=list(scratch),
        compiler_params=pltpu.CompilerParams(vmem_limit_bytes=limit),
        **specs,
    )


def two_parts(value):
    high = value.astype(BF).astype(F32)
    low = (value - high).astype(BF).astype(F32)
    return high, low


def block_body(age_ref, history_ref, cache_k_ref, span_k_ref, cache_v_ref, span_v_ref, out_ref):
    slots, width = cache_k_ref.shape
    tokens = span_k_ref.shape[0]
    live = slots + tokens
    out_ref[0:slots] = cache_k_ref[...]
    out_ref[slots:live] = span_k_ref[...]
    out_ref[KEYS : KEYS + slots] = cache_v_ref[...]
    out_ref[KEYS + slots : KEYS + live] = span_v_ref[...]
    out_ref[KEYS + live :] = jnp.zeros((KEYS - live, width), BF)
    valid = jnp.where(age_ref[...] < history_ref[0], 1.0, 0.0)
    flags = jnp.concatenate(
        [valid, jnp.ones((1, tokens), F32), jnp.zeros((1, width - live), F32)], axis=1
    )
    out_ref[live:KEYS] = jnp.broadcast_to(flags, (KEYS - live, width)).astype(BF)


def attend_body(q_ref, near_ref, far_ref, out_ref, *, heads, tokens, step):
    places = q_ref.shape[0]
    groups = tokens // 8
    rate = math.log2(math.e) / math.sqrt(HDIM)
    rows = step * tokens
    row = lax.broadcasted_iota(jnp.int32, (rows, 128), 0)
    lane = lax.broadcasted_iota(jnp.int32, (rows, 128), 1)
    group_lane = lane - heads * ((row % tokens) // 8)
    lane_key = lax.broadcasted_iota(jnp.int32, (2 * KEYS, HDIM), 1)
    value_tail = jnp.where(lane_key == 0, 1.0, 0.0).astype(BF)
    masks = []
    for ref in (near_ref, far_ref):
        flags = [ref[d, KEYS - 8 : KEYS, 0:KEYS].astype(F32)[0:1] for d in range(2)]
        masks.append((1.0 - jnp.concatenate(flags, axis=1)) * NEG)
    for head in range(heads):
        cols = slice(head * HDIM, (head + 1) * HDIM)
        keys = [ref[:, 0:KEYS, cols].reshape(2 * KEYS, HDIM) for ref in (near_ref, far_ref)]
        vals = [
            jnp.concatenate([ref[:, KEYS : 2 * KEYS, cols].reshape(2 * KEYS, HDIM), value_tail], axis=1)
            for ref in (near_ref, far_ref)
        ]
        for start in range(0, places, step):
            query = q_ref[start : start + step, :, cols].reshape(rows, HDIM)
            scores = [
                lax.dot_general(query, k, (((1,), (1,)), ((), ())), preferred_element_type=F32) + mask
                for k, mask in zip(keys, masks)
            ]
            top = jnp.max(jnp.maximum(scores[0], scores[1]), axis=1, keepdims=True)
            top_high, top_low = two_parts(top)
            top = top_high + top_low
            out = sum(
                jnp.dot(jnp.exp2((s - top) * rate).astype(BF), v, preferred_element_type=F32)
                for s, v in zip(scores, vals)
            )
            sum_high, sum_low = two_parts(out[:, HDIM : HDIM + 1])
            at = slice(head * tokens, (head + 1) * tokens)
            out_ref[start : start + step, at, :] = out[:, 0:HDIM].reshape(step, tokens, HDIM).astype(BF)
            stats = jnp.zeros((rows, 128), F32)
            for k, part in enumerate((top_high, top_low, sum_high, sum_low)):
                stats = jnp.where(group_lane == 32 * k + head, part, stats)
            folded = stats.reshape(step, groups, 8, 128).sum(axis=1)
            at = slice(heads * tokens, heads * tokens + 8)
            if head:
                folded = folded + out_ref[start : start + step, at, :].astype(F32)
            out_ref[start : start + step, at, :] = folded.astype(BF)


def merge_body(in_ref, out_ref, *, heads, tokens):
    groups = tokens // 8
    stats = in_ref[:, heads * tokens :, :].astype(F32)
    top = stats + pltpu.roll(stats, 96, 2)
    total = pltpu.roll(stats, 64, 2) + pltpu.roll(stats, 32, 2)
    peak = jnp.max(top, axis=0, keepdims=True)
    factor = jnp.exp((top - peak) * (1.0 / math.sqrt(HDIM)))
    lane = lax.broadcasted_iota(jnp.int32, (1, 8, 128), 2)
    total = jnp.where(lane < groups * heads, total, 1.0)
    factor = jnp.where(lane < groups * heads, factor, 1.0)
    share = factor / jnp.sum(factor * total, axis=0, keepdims=True)
    for head in range(heads):
        for group in range(groups):
            at = head * tokens + group * 8
            weight = share[:, :, group * heads + head : group * heads + head + 1]
            part = in_ref[:, at : at + 8, :].astype(F32) * weight
            out_ref[group * 8 : group * 8 + 8, head * HDIM : (head + 1) * HDIM] = jnp.sum(
                part, axis=0
            ).astype(BF)


def project_body(att_ref, weight_ref, out_ref, rows_ref, *, frames, token_rows):
    count = att_ref.shape[0]
    tokens = frames * token_rows
    chunks, rows, _ = out_ref.shape
    i = lax.broadcasted_iota(jnp.int32, (count, count), 0)
    j = lax.broadcasted_iota(jnp.int32, (count, count), 1)
    chunk = i % chunks
    source = (chunk // token_rows) * tokens + (i // chunks) * token_rows + chunk % token_rows
    order = jnp.where(j == source, 1.0, 0.0).astype(BF)
    att = jnp.dot(order, att_ref[...], preferred_element_type=F32).astype(BF)
    out = lax.dot_general(att, weight_ref[...], (((1,), (1,)), ((), ())), preferred_element_type=F32)
    blocks = out.shape[1] // 128
    for block in range(blocks):
        for frame in range(frames):
            rows_ref[pl.ds(block * frames + frame, chunks, stride=rows), :] = out[
                frame * chunks : (frame + 1) * chunks, block * 128 : (block + 1) * 128
            ]
    for row in range(blocks * frames, rows):
        rows_ref[pl.ds(row, chunks, stride=rows), :] = jnp.zeros((chunks, 128), F32)
    out_ref[...] = rows_ref[...].reshape(chunks, rows, 128).astype(BF)


def head_body(
    in_ref, stream_ref, gate_ref, shift_ref, scale_ref, weight_ref, stream_out_ref, patch_ref, sum_ref, *, blocks, places
):
    parts = in_ref.shape[0] // blocks
    frames, features = stream_ref.shape
    size = features // blocks
    width = size // places
    for block in range(blocks):
        total = in_ref[block * parts].astype(F32)
        for k in range(1, parts):
            total = total + in_ref[block * parts + k].astype(F32)
        total = jnp.concatenate([total[k * frames : (k + 1) * frames] for k in range(size // 128)], axis=1)
        outer, inner = block // 2, block % 2
        for place in range(places):
            at = ((outer * places + place) * 2 + inner) * width
            sum_ref[:, at : at + width] = total[:, place * width : (place + 1) * width]
    mixed = (stream_ref[...].astype(F32) + gate_ref[...] * sum_ref[...]).astype(BF)
    stream_out_ref[...] = mixed
    mixed = mixed.astype(F32)
    mean = jnp.mean(mixed, axis=-1, keepdims=True)
    centred = mixed - mean
    variance = jnp.mean(centred * centred, axis=-1, keepdims=True)
    normed = (centred * lax.rsqrt(variance + 1e-06) * (1.0 + scale_ref[...]) + shift_ref[...]).astype(BF)
    patch_ref[...] = lax.dot_general(
        normed, weight_ref[...], (((1,), (1,)), ((), ())), preferred_element_type=F32
    ).astype(BF)


def conv_body(in_ref, weight_ref, gain_ref, out_ref, patch_ref, *, frames, token_rows):
    core = lax.axis_index("core")
    row = lax.axis_index("y") * 2 + lax.axis_index("xh")

    def cells(at_core, at_row):
        found = in_ref[at_core * token_rows + jnp.clip(at_row, 0, token_rows - 1)].astype(F32)
        return jnp.where((at_row >= 0) & (at_row < token_rows), found, 0.0)

    by_col = [[], [], []]
    half = in_ref.shape[2] // 2
    for step in (-1, 0, 1):
        mine, other = cells(core, row + step), cells(1 - core, row + step)
        beside, across = other[:, 0:half], mine[:, half:]
        by_col[0].append(jnp.where(core == 1, beside, across))
        by_col[1].append(mine[:, 0:half])
        by_col[2].append(jnp.where(core == 1, across, beside))
    for a in range(PATCH):
        for b in range(PATCH):
            pieces = []
            for u in range(3):
                for v in range(3):
                    for w in range(3):
                        i, j = a + v - 1, b + w - 1
                        block = by_col[j // 2 + 1][i // 2 + 1]
                        at = ((i % 2) * 2 + (j % 2)) * LAT
                        pieces.append(block[u : u + frames, at : at + LAT])
            patch_ref[(a * 2 + b) * 8 : (a * 2 + b) * 8 + frames, :] = jnp.concatenate(pieces, axis=1)
    patches = patch_ref[...].astype(BF)
    conv = jnp.dot(patches, weight_ref[...], preferred_element_type=F32)
    square = jnp.mean(conv * conv, axis=-1, keepdims=True)
    scaled = conv * lax.rsqrt(square + 1e-06) * gain_ref[...]
    silu = (scaled / (1.0 + jnp.exp(-scaled))).astype(BF)
    for f in range(frames):
        for a in range(PATCH):
            for b in range(PATCH):
                at = (a * 2 + b) * 8 + f
                out_ref[f, a, b : b + 1, :] = silu[at : at + 1, :]


COL = ("xl", "z", "core")
ROW = ("y", "xh")


def local(
    stream,
    queries,
    span_k,
    span_v,
    cache_k,
    cache_v,
    cache_age,
    history,
    out_weight,
    attn_gate,
    head_shift,
    head_scale,
    head_weight,
    latent_cache,
    conv_weight,
    rms_gain,
):
    frames, token_rows, _, width = queries.shape
    tokens = frames * token_rows
    heads = width // HDIM
    places = lax.axis_size("z")
    features = stream.shape[-1]

    weights = lax.all_gather(out_weight.T, "z", axis=0, tiled=True)

    own = full_call(
        block_body,
        jax.ShapeDtypeStruct((2 * KEYS, width), BF),
        limit=None,
        in_specs=[pl.BlockSpec(), pl.BlockSpec(memory_space=pltpu.SMEM)] + [pl.BlockSpec()] * 4,
    )(
        cache_age[None, :],
        history,
        cache_k,
        span_k.reshape(tokens, width),
        cache_v,
        span_v.reshape(tokens, width),
    )
    near = lax.all_gather(own, "core", axis=0)
    far = lax.ppermute(near, "xl", [(0, 1), (1, 0)])
    gathered = lax.all_gather(queries.reshape(tokens, width), "z", axis=0)
    partial = full_call(
        functools.partial(attend_body, heads=heads, tokens=tokens, step=8),
        jax.ShapeDtypeStruct((places, heads * tokens + 8, HDIM), BF),
    )(gathered, near, far)
    partial = lax.all_to_all(partial, "z", 0, 0, tiled=True)
    attended = full_call(
        functools.partial(merge_body, heads=heads, tokens=tokens),
        jax.ShapeDtypeStruct((tokens, width), BF),
    )(partial)
    group = lax.all_gather(attended, ("xl", "core"), axis=0, tiled=True)
    terms = full_call(
        functools.partial(project_body, frames=frames, token_rows=token_rows),
        jax.ShapeDtypeStruct((4 * token_rows, 32, 128), BF),
        [pltpu.VMEM((4 * token_rows * 32, 128), F32)],
    )(group, weights)
    terms = lax.all_to_all(terms, ("xl", "core") + ROW, 0, 0, tiled=True)
    stream_out, patch = full_call(
        functools.partial(head_body, blocks=4, places=places),
        (
            jax.ShapeDtypeStruct((frames, features), BF),
            jax.ShapeDtypeStruct((frames, head_weight.shape[1]), BF),
        ),
        [pltpu.VMEM((frames, features), F32)],
    )(
        terms,
        stream.reshape(frames, features),
        attn_gate[None, :],
        head_shift[None, :],
        head_scale[None, :],
        head_weight.T,
    )
    cells = jnp.concatenate([latent_cache.reshape(2, -1), patch], axis=0)
    pairs = [(i, i + 1) for i in range(1, 63, 2)]
    across = lax.ppermute(cells, COL, pairs + [(j, i) for i, j in pairs])
    cells = jnp.pad(jnp.concatenate([cells, across], axis=1), ((0, 8 - cells.shape[0]), (0, 0)))
    cells = jnp.broadcast_to(cells[None], (2 * token_rows,) + cells.shape)
    cells = lax.all_to_all(cells, ("core",) + ROW, 0, 0, tiled=True)
    decoded = full_call(
        functools.partial(conv_body, frames=frames, token_rows=token_rows),
        jax.ShapeDtypeStruct((frames, PATCH, PATCH, conv_weight.shape[1]), BF),
        [pltpu.VMEM((32, conv_weight.shape[0]), F32)],
    )(cells, conv_weight, rms_gain[None, :])
    return stream_out.reshape(stream.shape), decoded


def solution(mesh):
    fine = Mesh(mesh.devices.reshape(2, 16, 2, 4, 2), COL + ROW)
    placed = (
        P(None, ROW, COL, None),
        P(None, None, COL, ROW),
        P(None, None, COL, ROW),
        P(None, None, COL, ROW),
        P(COL, ROW),
        P(COL, ROW),
        P(COL),
        P(),
        P(ROW, COL),
        P(),
        P(),
        P(),
        P(),
        P(None, ROW, COL, None),
        P(),
        P(),
    )
    return jax.shard_map(
        local,
        mesh=fine,
        in_specs=placed,
        out_specs=(P(None, ROW, COL, None), P(None, ROW, COL, None)),
        check_vma=False,
    )
```

```python
import functools
import math

import jax
import jax.numpy as jnp
from jax import lax
from jax.experimental import pallas as pl
from jax.experimental.pallas import tpu as pltpu
from jax.sharding import Mesh
from jax.sharding import PartitionSpec as P

HDIM = 128
LAT = 16
PATCH = 2
KEYS = 128
NEG = -1e30


BF = jnp.bfloat16
F32 = jnp.float32


def full_call(body, out_shape, scratch=(), limit=24 * 1024 * 1024, **specs):
    return pl.pallas_call(
        body,
        out_shape=out_shape,
        scratch_shapes=list(scratch),
        compiler_params=pltpu.CompilerParams(vmem_limit_bytes=limit),
        **specs,
    )


def two_parts(value):
    high = value.astype(BF).astype(F32)
    low = (value - high).astype(BF).astype(F32)
    return high, low


def block_body(age_ref, history_ref, cache_k_ref, span_k_ref, cache_v_ref, span_v_ref, out_ref):
    slots, width = cache_k_ref.shape
    tokens = span_k_ref.shape[0]
    live = slots + tokens
    out_ref[0:slots] = cache_k_ref[...]
    out_ref[slots:live] = span_k_ref[...]
    out_ref[KEYS : KEYS + slots] = cache_v_ref[...]
    out_ref[KEYS + slots : KEYS + live] = span_v_ref[...]
    out_ref[KEYS + live :] = jnp.zeros((KEYS - live, width), BF)
    valid = jnp.where(age_ref[...] < history_ref[0], 1.0, 0.0)
    flags = jnp.concatenate(
        [valid, jnp.ones((1, tokens), F32), jnp.zeros((1, width - live), F32)], axis=1
    )
    out_ref[live:KEYS] = jnp.broadcast_to(flags, (KEYS - live, width)).astype(BF)


def attend_body(q_ref, near_ref, far_ref, out_ref, *, heads, tokens, step):
    places = q_ref.shape[0]
    groups = tokens // 8
    rate = math.log2(math.e) / math.sqrt(HDIM)
    rows = step * tokens
    row = lax.broadcasted_iota(jnp.int32, (rows, 128), 0)
    lane = lax.broadcasted_iota(jnp.int32, (rows, 128), 1)
    group_lane = lane - heads * ((row % tokens) // 8)
    lane_key = lax.broadcasted_iota(jnp.int32, (2 * KEYS, HDIM), 1)
    value_tail = jnp.where(lane_key == 0, 1.0, 0.0).astype(BF)
    masks = []
    for ref in (near_ref, far_ref):
        flags = [ref[d, KEYS - 8 : KEYS, 0:KEYS].astype(F32)[0:1] for d in range(2)]
        masks.append((1.0 - jnp.concatenate(flags, axis=1)) * NEG)
    for head in range(heads):
        cols = slice(head * HDIM, (head + 1) * HDIM)
        keys = [ref[:, 0:KEYS, cols].reshape(2 * KEYS, HDIM) for ref in (near_ref, far_ref)]
        vals = [
            jnp.concatenate([ref[:, KEYS : 2 * KEYS, cols].reshape(2 * KEYS, HDIM), value_tail], axis=1)
            for ref in (near_ref, far_ref)
        ]
        for start in range(0, places, step):
            query = q_ref[start : start + step, :, cols].reshape(rows, HDIM)
            scores = [
                lax.dot_general(query, k, (((1,), (1,)), ((), ())), preferred_element_type=F32) + mask
                for k, mask in zip(keys, masks)
            ]
            top = jnp.max(jnp.maximum(scores[0], scores[1]), axis=1, keepdims=True)
            top_high, top_low = two_parts(top)
            top = top_high + top_low
            out = sum(
                jnp.dot(jnp.exp2((s - top) * rate).astype(BF), v, preferred_element_type=F32)
                for s, v in zip(scores, vals)
            )
            sum_high, sum_low = two_parts(out[:, HDIM : HDIM + 1])
            at = slice(head * tokens, (head + 1) * tokens)
            out_ref[start : start + step, at, :] = out[:, 0:HDIM].reshape(step, tokens, HDIM).astype(BF)
            stats = jnp.zeros((rows, 128), F32)
            for k, part in enumerate((top_high, top_low, sum_high, sum_low)):
                stats = jnp.where(group_lane == 32 * k + head, part, stats)
            folded = stats.reshape(step, groups, 8, 128).sum(axis=1)
            at = slice(heads * tokens, heads * tokens + 8)
            if head:
                folded = folded + out_ref[start : start + step, at, :].astype(F32)
            out_ref[start : start + step, at, :] = folded.astype(BF)


def merge_body(in_ref, out_ref, *, heads, tokens):
    groups = tokens // 8
    stats = in_ref[:, heads * tokens :, :].astype(F32)
    top = stats + pltpu.roll(stats, 96, 2)
    total = pltpu.roll(stats, 64, 2) + pltpu.roll(stats, 32, 2)
    peak = jnp.max(top, axis=0, keepdims=True)
    factor = jnp.exp((top - peak) * (1.0 / math.sqrt(HDIM)))
    lane = lax.broadcasted_iota(jnp.int32, (1, 8, 128), 2)
    total = jnp.where(lane < groups * heads, total, 1.0)
    factor = jnp.where(lane < groups * heads, factor, 1.0)
    share = factor / jnp.sum(factor * total, axis=0, keepdims=True)
    for head in range(heads):
        for group in range(groups):
            at = head * tokens + group * 8
            weight = share[:, :, group * heads + head : group * heads + head + 1]
            part = in_ref[:, at : at + 8, :].astype(F32) * weight
            out_ref[group * 8 : group * 8 + 8, head * HDIM : (head + 1) * HDIM] = jnp.sum(
                part, axis=0
            ).astype(BF)


def project_body(att_ref, weight_ref, out_ref, rows_ref, *, frames, token_rows):
    count = att_ref.shape[0]
    tokens = frames * token_rows
    chunks, rows, _ = out_ref.shape
    i = lax.broadcasted_iota(jnp.int32, (count, count), 0)
    j = lax.broadcasted_iota(jnp.int32, (count, count), 1)
    chunk = i % chunks
    source = (chunk // token_rows) * tokens + (i // chunks) * token_rows + chunk % token_rows
    order = jnp.where(j == source, 1.0, 0.0).astype(BF)
    att = jnp.dot(order, att_ref[...], preferred_element_type=F32).astype(BF)
    out = lax.dot_general(att, weight_ref[...], (((1,), (1,)), ((), ())), preferred_element_type=F32)
    blocks = out.shape[1] // 128
    for block in range(blocks):
        for frame in range(frames):
            rows_ref[pl.ds(block * frames + frame, chunks, stride=rows), :] = out[
                frame * chunks : (frame + 1) * chunks, block * 128 : (block + 1) * 128
            ]
    for row in range(blocks * frames, rows):
        rows_ref[pl.ds(row, chunks, stride=rows), :] = jnp.zeros((chunks, 128), F32)
    out_ref[...] = rows_ref[...].reshape(chunks, rows, 128).astype(BF)


def head_body(
    in_ref, stream_ref, gate_ref, shift_ref, scale_ref, weight_ref, cache_ref, stream_out_ref, cells_ref, sum_ref, *, blocks, places
):
    parts = in_ref.shape[0] // blocks
    frames, features = stream_ref.shape
    size = features // blocks
    width = size // places
    for block in range(blocks):
        total = in_ref[block * parts].astype(F32)
        for k in range(1, parts):
            total = total + in_ref[block * parts + k].astype(F32)
        total = jnp.concatenate([total[k * frames : (k + 1) * frames] for k in range(size // 128)], axis=1)
        outer, inner = block // 2, block % 2
        for place in range(places):
            at = ((outer * places + place) * 2 + inner) * width
            sum_ref[:, at : at + width] = total[:, place * width : (place + 1) * width]
    mixed = (stream_ref[...].astype(F32) + gate_ref[...] * sum_ref[...]).astype(BF)
    stream_out_ref[...] = mixed
    mixed = mixed.astype(F32)
    mean = jnp.mean(mixed, axis=-1, keepdims=True)
    centred = mixed - mean
    variance = jnp.mean(centred * centred, axis=-1, keepdims=True)
    normed = (centred * lax.rsqrt(variance + 1e-06) * (1.0 + scale_ref[...]) + shift_ref[...]).astype(BF)
    patch = lax.dot_general(
        normed, weight_ref[...], (((1,), (1,)), ((), ())), preferred_element_type=F32
    ).astype(BF)
    peers, rows, lanes = cells_ref.shape
    cells = jnp.concatenate([cache_ref[...].astype(F32), patch.astype(F32)], axis=0)
    cells = jnp.concatenate([cells, jnp.zeros((rows - cells.shape[0], cells.shape[1]), F32)], axis=0)
    cells = jnp.concatenate([cells, jnp.zeros((rows, lanes - cells.shape[1]), F32)], axis=1)
    cells_ref[...] = jnp.broadcast_to(cells[None], cells_ref.shape).astype(BF)


def conv_body(in_ref, weight_ref, gain_ref, out_ref, patch_ref, *, frames, token_rows, cols):
    core = lax.axis_index("core")
    col = lax.axis_index("xl") * (cols // 2) + lax.axis_index("z") * 2 + core
    row = lax.axis_index("y") * 2 + lax.axis_index("xh")
    inner = (col > 0) & (col < cols - 1)

    def cells(at_core, place, at_row, exists):
        found = in_ref[at_core, place * token_rows + jnp.clip(at_row, 0, token_rows - 1)].astype(F32)
        return jnp.where((at_row >= 0) & (at_row < token_rows) & exists, found, 0.0)

    by_col = [[], [], []]
    for step in (-1, 0, 1):
        beside = cells(1 - core, core, row + step, True)
        across = cells(core, core, row + step, inner)
        by_col[0].append(jnp.where(core == 1, beside, across))
        by_col[1].append(cells(core, 1 - core, row + step, True))
        by_col[2].append(jnp.where(core == 1, across, beside))
    for a in range(PATCH):
        for b in range(PATCH):
            pieces = []
            for u in range(3):
                for v in range(3):
                    for w in range(3):
                        i, j = a + v - 1, b + w - 1
                        block = by_col[j // 2 + 1][i // 2 + 1]
                        at = ((i % 2) * 2 + (j % 2)) * LAT
                        pieces.append(block[u : u + frames, at : at + LAT])
            patch_ref[(a * 2 + b) * 8 : (a * 2 + b) * 8 + frames, :] = jnp.concatenate(pieces, axis=1)
    patches = patch_ref[...].astype(BF)
    conv = jnp.dot(patches, weight_ref[...], preferred_element_type=F32)
    square = jnp.mean(conv * conv, axis=-1, keepdims=True)
    scaled = conv * lax.rsqrt(square + 1e-06) * gain_ref[...]
    silu = (scaled / (1.0 + jnp.exp(-scaled))).astype(BF)
    for f in range(frames):
        for a in range(PATCH):
            for b in range(PATCH):
                at = (a * 2 + b) * 8 + f
                out_ref[f, a, b : b + 1, :] = silu[at : at + 1, :]


COL = ("xl", "z", "core")
ROW = ("y", "xh")


def local(
    stream,
    queries,
    span_k,
    span_v,
    cache_k,
    cache_v,
    cache_age,
    history,
    out_weight,
    attn_gate,
    head_shift,
    head_scale,
    head_weight,
    latent_cache,
    conv_weight,
    rms_gain,
):
    frames, token_rows, _, width = queries.shape
    tokens = frames * token_rows
    heads = width // HDIM
    places = lax.axis_size("z")
    features = stream.shape[-1]

    weights = lax.all_gather(out_weight.T, "z", axis=0, tiled=True)

    own = full_call(
        block_body,
        jax.ShapeDtypeStruct((2 * KEYS, width), BF),
        limit=None,
        in_specs=[pl.BlockSpec(), pl.BlockSpec(memory_space=pltpu.SMEM)] + [pl.BlockSpec()] * 4,
    )(
        cache_age[None, :],
        history,
        cache_k,
        span_k.reshape(tokens, width),
        cache_v,
        span_v.reshape(tokens, width),
    )
    near = lax.all_gather(own, "core", axis=0)
    far = lax.ppermute(near, "xl", [(0, 1), (1, 0)])
    gathered = lax.all_gather(queries.reshape(tokens, width), "z", axis=0)
    partial = full_call(
        functools.partial(attend_body, heads=heads, tokens=tokens, step=8),
        jax.ShapeDtypeStruct((places, heads * tokens + 8, HDIM), BF),
    )(gathered, near, far)
    partial = lax.all_to_all(partial, "z", 0, 0, tiled=True)
    attended = full_call(
        functools.partial(merge_body, heads=heads, tokens=tokens),
        jax.ShapeDtypeStruct((tokens, width), BF),
    )(partial)
    group = lax.all_gather(attended, ("xl", "core"), axis=0, tiled=True)
    terms = full_call(
        functools.partial(project_body, frames=frames, token_rows=token_rows),
        jax.ShapeDtypeStruct((4 * token_rows, 32, 128), BF),
        [pltpu.VMEM((4 * token_rows * 32, 128), F32)],
    )(group, weights)
    terms = lax.all_to_all(terms, ("xl", "core") + ROW, 0, 0, tiled=True)
    stream_out, cells = full_call(
        functools.partial(head_body, blocks=4, places=places),
        (
            jax.ShapeDtypeStruct((frames, features), BF),
            jax.ShapeDtypeStruct((2 * token_rows, 8, 128), BF),
        ),
        [pltpu.VMEM((frames, features), F32)],
    )(
        terms,
        stream.reshape(frames, features),
        attn_gate[None, :],
        head_shift[None, :],
        head_scale[None, :],
        head_weight.T,
        latent_cache.reshape(2, -1),
    )
    cols = 2 * lax.axis_size("xl") * places
    starts = [(k, k + 1) for k in range(1, cols - 1, 2)] + [(cols - 1, 0)]
    pairs = [[c * token_rows + r for c in pair for r in range(token_rows)] for pair in starts]
    cells = lax.all_to_all(cells, COL + ROW, 0, 0, tiled=True, axis_index_groups=pairs)
    cells = lax.all_gather(cells, "core", axis=0)
    decoded = full_call(
        functools.partial(conv_body, frames=frames, token_rows=token_rows, cols=cols),
        jax.ShapeDtypeStruct((frames, PATCH, PATCH, conv_weight.shape[1]), BF),
        [pltpu.VMEM((32, conv_weight.shape[0]), F32)],
    )(cells, conv_weight, rms_gain[None, :])
    return stream_out.reshape(stream.shape), decoded


def solution(mesh):
    fine = Mesh(mesh.devices.reshape(2, 16, 2, 4, 2), COL + ROW)
    placed = (
        P(None, ROW, COL, None),
        P(None, None, COL, ROW),
        P(None, None, COL, ROW),
        P(None, None, COL, ROW),
        P(COL, ROW),
        P(COL, ROW),
        P(COL),
        P(),
        P(ROW, COL),
        P(),
        P(),
        P(),
        P(),
        P(None, ROW, COL, None),
        P(),
        P(),
    )
    return jax.shard_map(
        local,
        mesh=fine,
        in_specs=placed,
        out_specs=(P(None, ROW, COL, None), P(None, ROW, COL, None)),
        check_vma=False,
    )
```

```python
import functools
import math

import jax
import jax.numpy as jnp
from jax import lax
from jax.experimental import pallas as pl
from jax.experimental.pallas import tpu as pltpu
from jax.sharding import Mesh
from jax.sharding import PartitionSpec as P

HDIM = 128
LAT = 16
PATCH = 2
KEYS = 128
NEG = -1e30


BF = jnp.bfloat16
F32 = jnp.float32


def full_call(body, out_shape, scratch=(), limit=24 * 1024 * 1024, **specs):
    return pl.pallas_call(
        body,
        out_shape=out_shape,
        scratch_shapes=list(scratch),
        compiler_params=pltpu.CompilerParams(vmem_limit_bytes=limit),
        **specs,
    )


def two_parts(value):
    high = value.astype(BF).astype(F32)
    low = (value - high).astype(BF).astype(F32)
    return high, low


def block_body(age_ref, history_ref, cache_k_ref, span_k_ref, cache_v_ref, span_v_ref, out_ref):
    slots, width = cache_k_ref.shape
    tokens = span_k_ref.shape[0]
    live = slots + tokens
    out_ref[0:slots] = cache_k_ref[...]
    out_ref[slots:live] = span_k_ref[...]
    out_ref[KEYS : KEYS + slots] = cache_v_ref[...]
    out_ref[KEYS + slots : KEYS + live] = span_v_ref[...]
    out_ref[KEYS + live :] = jnp.zeros((KEYS - live, width), BF)
    valid = jnp.where(age_ref[...] < history_ref[0], 1.0, 0.0)
    flags = jnp.concatenate(
        [valid, jnp.ones((1, tokens), F32), jnp.zeros((1, width - live), F32)], axis=1
    )
    out_ref[live:KEYS] = jnp.broadcast_to(flags, (KEYS - live, width)).astype(BF)


def attend_body(q_ref, near_ref, far_ref, out_ref, *, heads, tokens, step):
    places = q_ref.shape[0]
    groups = tokens // 8
    rate = math.log2(math.e) / math.sqrt(HDIM)
    rows = step * tokens
    row = lax.broadcasted_iota(jnp.int32, (rows, 128), 0)
    lane = lax.broadcasted_iota(jnp.int32, (rows, 128), 1)
    group_lane = lane - heads * ((row % tokens) // 8)
    lane_key = lax.broadcasted_iota(jnp.int32, (2 * KEYS, HDIM), 1)
    value_tail = jnp.where(lane_key == 0, 1.0, 0.0).astype(BF)
    masks = []
    for ref in (near_ref, far_ref):
        flags = [ref[d, KEYS - 8 : KEYS, 0:KEYS].astype(F32)[0:1] for d in range(2)]
        masks.append((1.0 - jnp.concatenate(flags, axis=1)) * NEG)
    for head in range(heads):
        cols = slice(head * HDIM, (head + 1) * HDIM)
        keys = [ref[:, 0:KEYS, cols].reshape(2 * KEYS, HDIM) for ref in (near_ref, far_ref)]
        vals = [
            jnp.concatenate([ref[:, KEYS : 2 * KEYS, cols].reshape(2 * KEYS, HDIM), value_tail], axis=1)
            for ref in (near_ref, far_ref)
        ]
        for start in range(0, places, step):
            query = q_ref[start : start + step, :, cols].reshape(rows, HDIM)
            scores = [
                lax.dot_general(query, k, (((1,), (1,)), ((), ())), preferred_element_type=F32) + mask
                for k, mask in zip(keys, masks)
            ]
            top = jnp.max(jnp.maximum(scores[0], scores[1]), axis=1, keepdims=True)
            top_high, top_low = two_parts(top)
            top = top_high + top_low
            out = sum(
                jnp.dot(jnp.exp2((s - top) * rate).astype(BF), v, preferred_element_type=F32)
                for s, v in zip(scores, vals)
            )
            sum_high, sum_low = two_parts(out[:, HDIM : HDIM + 1])
            at = slice(head * tokens, (head + 1) * tokens)
            out_ref[start : start + step, at, :] = out[:, 0:HDIM].reshape(step, tokens, HDIM).astype(BF)
            stats = jnp.zeros((rows, 128), F32)
            for k, part in enumerate((top_high, top_low, sum_high, sum_low)):
                stats = jnp.where(group_lane == 32 * k + head, part, stats)
            folded = stats.reshape(step, groups, 8, 128).sum(axis=1)
            at = slice(heads * tokens, heads * tokens + 8)
            if head:
                folded = folded + out_ref[start : start + step, at, :].astype(F32)
            out_ref[start : start + step, at, :] = folded.astype(BF)


def merge_body(in_ref, out_ref, *, heads, tokens):
    groups = tokens // 8
    stats = in_ref[:, heads * tokens :, :].astype(F32)
    top = stats + pltpu.roll(stats, 96, 2)
    total = pltpu.roll(stats, 64, 2) + pltpu.roll(stats, 32, 2)
    peak = jnp.max(top, axis=0, keepdims=True)
    factor = jnp.exp((top - peak) * (1.0 / math.sqrt(HDIM)))
    lane = lax.broadcasted_iota(jnp.int32, (1, 8, 128), 2)
    total = jnp.where(lane < groups * heads, total, 1.0)
    factor = jnp.where(lane < groups * heads, factor, 1.0)
    share = factor / jnp.sum(factor * total, axis=0, keepdims=True)
    for head in range(heads):
        for group in range(groups):
            at = head * tokens + group * 8
            weight = share[:, :, group * heads + head : group * heads + head + 1]
            part = in_ref[:, at : at + 8, :].astype(F32) * weight
            out_ref[group * 8 : group * 8 + 8, head * HDIM : (head + 1) * HDIM] = jnp.sum(
                part, axis=0
            ).astype(BF)


def project_body(att_ref, weight_ref, out_ref, rows_ref, *, frames, token_rows):
    count = att_ref.shape[0]
    tokens = frames * token_rows
    chunks, rows, _ = out_ref.shape
    i = lax.broadcasted_iota(jnp.int32, (count, count), 0)
    j = lax.broadcasted_iota(jnp.int32, (count, count), 1)
    chunk = i % chunks
    source = (chunk // token_rows) * tokens + (i // chunks) * token_rows + chunk % token_rows
    order = jnp.where(j == source, 1.0, 0.0).astype(BF)
    att = jnp.dot(order, att_ref[...], preferred_element_type=F32).astype(BF)
    out = lax.dot_general(att, weight_ref[...], (((1,), (1,)), ((), ())), preferred_element_type=F32)
    blocks = out.shape[1] // 128
    for block in range(blocks):
        for frame in range(frames):
            rows_ref[pl.ds(block * frames + frame, chunks, stride=rows), :] = out[
                frame * chunks : (frame + 1) * chunks, block * 128 : (block + 1) * 128
            ]
    for row in range(blocks * frames, rows):
        rows_ref[pl.ds(row, chunks, stride=rows), :] = jnp.zeros((chunks, 128), F32)
    out_ref[...] = rows_ref[...].reshape(chunks, rows, 128).astype(BF)


def head_body(
    in_ref, stream_ref, gate_ref, shift_ref, scale_ref, weight_ref, cache_ref, stream_out_ref, cells_ref, sum_ref, *, blocks
):
    parts = in_ref.shape[0] // blocks
    frames, features = stream_ref.shape
    size = features // blocks
    for block in range(blocks):
        total = in_ref[block * parts].astype(F32)
        for k in range(1, parts):
            total = total + in_ref[block * parts + k].astype(F32)
        total = jnp.concatenate([total[k * frames : (k + 1) * frames] for k in range(size // 128)], axis=1)
        sum_ref[:, block * size : (block + 1) * size] = total
    mixed = (stream_ref[...].astype(F32) + gate_ref[...] * sum_ref[...]).astype(BF)
    stream_out_ref[...] = mixed
    mixed = mixed.astype(F32)
    mean = jnp.mean(mixed, axis=-1, keepdims=True)
    centred = mixed - mean
    variance = jnp.mean(centred * centred, axis=-1, keepdims=True)
    normed = (centred * lax.rsqrt(variance + 1e-06) * (1.0 + scale_ref[...]) + shift_ref[...]).astype(BF)
    patch = lax.dot_general(
        normed, weight_ref[...], (((1,), (1,)), ((), ())), preferred_element_type=F32
    ).astype(BF)
    peers, rows, lanes = cells_ref.shape
    cells = jnp.concatenate([cache_ref[...].astype(F32), patch.astype(F32)], axis=0)
    cells = jnp.concatenate([cells, jnp.zeros((rows - cells.shape[0], cells.shape[1]), F32)], axis=0)
    cells = jnp.concatenate([cells, jnp.zeros((rows, lanes - cells.shape[1]), F32)], axis=1)
    cells_ref[...] = jnp.broadcast_to(cells[None], cells_ref.shape).astype(BF)


def conv_body(in_ref, weight_ref, gain_ref, out_ref, patch_ref, *, frames, token_rows, cols):
    core = lax.axis_index("core")
    col = lax.axis_index("xl") * (cols // 2) + lax.axis_index("z") * 2 + core
    row = lax.axis_index("y") * 2 + lax.axis_index("xh")
    inner = (col > 0) & (col < cols - 1)

    def cells(at_core, place, at_row, exists):
        found = in_ref[at_core, place * token_rows + jnp.clip(at_row, 0, token_rows - 1)].astype(F32)
        return jnp.where((at_row >= 0) & (at_row < token_rows) & exists, found, 0.0)

    by_col = [[], [], []]
    for step in (-1, 0, 1):
        beside = cells(1 - core, core, row + step, True)
        across = cells(core, core, row + step, inner)
        by_col[0].append(jnp.where(core == 1, beside, across))
        by_col[1].append(cells(core, 1 - core, row + step, True))
        by_col[2].append(jnp.where(core == 1, across, beside))
    for a in range(PATCH):
        for b in range(PATCH):
            pieces = []
            for u in range(3):
                for v in range(3):
                    for w in range(3):
                        i, j = a + v - 1, b + w - 1
                        block = by_col[j // 2 + 1][i // 2 + 1]
                        at = ((i % 2) * 2 + (j % 2)) * LAT
                        pieces.append(block[u : u + frames, at : at + LAT])
            patch_ref[(a * 2 + b) * 8 : (a * 2 + b) * 8 + frames, :] = jnp.concatenate(pieces, axis=1)
    patches = patch_ref[...].astype(BF)
    conv = jnp.dot(patches, weight_ref[...], preferred_element_type=F32)
    square = jnp.mean(conv * conv, axis=-1, keepdims=True)
    scaled = conv * lax.rsqrt(square + 1e-06) * gain_ref[...]
    silu = (scaled / (1.0 + jnp.exp(-scaled))).astype(BF)
    for f in range(frames):
        for a in range(PATCH):
            for b in range(PATCH):
                at = (a * 2 + b) * 8 + f
                out_ref[f, a, b : b + 1, :] = silu[at : at + 1, :]


COL = ("xl", "z", "core")
ROW = ("y", "xh")


def local(
    stream,
    queries,
    span_k,
    span_v,
    cache_k,
    cache_v,
    cache_age,
    history,
    out_weight,
    attn_gate,
    head_shift,
    head_scale,
    head_weight,
    latent_cache,
    conv_weight,
    rms_gain,
):
    frames, token_rows, _, width = queries.shape
    tokens = frames * token_rows
    heads = width // HDIM
    places = lax.axis_size("z")
    features = stream.shape[-1]

    weights = lax.all_gather(out_weight.T, ("z", "core"), axis=0, tiled=True)

    own = full_call(
        block_body,
        jax.ShapeDtypeStruct((2 * KEYS, width), BF),
        limit=None,
        in_specs=[pl.BlockSpec(), pl.BlockSpec(memory_space=pltpu.SMEM)] + [pl.BlockSpec()] * 4,
    )(
        cache_age[None, :],
        history,
        cache_k,
        span_k.reshape(tokens, width),
        cache_v,
        span_v.reshape(tokens, width),
    )
    near = lax.all_gather(own, "core", axis=0)
    far = lax.ppermute(near, "xl", [(0, 1), (1, 0)])
    gathered = lax.all_gather(queries.reshape(tokens, width), "z", axis=0)
    partial = full_call(
        functools.partial(attend_body, heads=heads, tokens=tokens, step=8),
        jax.ShapeDtypeStruct((places, heads * tokens + 8, HDIM), BF),
    )(gathered, near, far)
    partial = lax.all_to_all(partial, "z", 0, 0, tiled=True)
    attended = full_call(
        functools.partial(merge_body, heads=heads, tokens=tokens),
        jax.ShapeDtypeStruct((tokens, width), BF),
    )(partial)
    group = lax.all_gather(attended, "xl", axis=0, tiled=True)
    terms = full_call(
        functools.partial(project_body, frames=frames, token_rows=token_rows),
        jax.ShapeDtypeStruct((2 * token_rows, 64, 128), BF),
        [pltpu.VMEM((2 * token_rows * 64, 128), F32)],
    )(group, weights)
    terms = lax.all_to_all(terms, ("xl",) + ROW, 0, 0, tiled=True)
    stream_out, cells = full_call(
        functools.partial(head_body, blocks=2),
        (
            jax.ShapeDtypeStruct((frames, features), BF),
            jax.ShapeDtypeStruct((2 * token_rows, 8, 128), BF),
        ),
        [pltpu.VMEM((frames, features), F32)],
    )(
        terms,
        stream.reshape(frames, features),
        attn_gate[None, :],
        head_shift[None, :],
        head_scale[None, :],
        head_weight.T,
        latent_cache.reshape(2, -1),
    )
    cols = 2 * lax.axis_size("xl") * places
    starts = [(k, k + 1) for k in range(1, cols - 1, 2)] + [(cols - 1, 0)]
    pairs = [[c * token_rows + r for c in pair for r in range(token_rows)] for pair in starts]
    cells = lax.all_to_all(cells, COL + ROW, 0, 0, tiled=True, axis_index_groups=pairs)
    cells = lax.all_gather(cells, "core", axis=0)
    decoded = full_call(
        functools.partial(conv_body, frames=frames, token_rows=token_rows, cols=cols),
        jax.ShapeDtypeStruct((frames, PATCH, PATCH, conv_weight.shape[1]), BF),
        [pltpu.VMEM((32, conv_weight.shape[0]), F32)],
    )(cells, conv_weight, rms_gain[None, :])
    return stream_out.reshape(stream.shape), decoded


def solution(mesh):
    fine = Mesh(mesh.devices.reshape(2, 16, 2, 4, 2), COL + ROW)
    placed = (
        P(None, ROW, COL, None),
        P(None, None, COL, ROW),
        P(None, None, COL, ROW),
        P(None, None, COL, ROW),
        P(COL, ROW),
        P(COL, ROW),
        P(COL),
        P(),
        P(ROW, COL),
        P(),
        P(),
        P(),
        P(),
        P(None, ROW, COL, None),
        P(),
        P(),
    )
    return jax.shard_map(
        local,
        mesh=fine,
        in_specs=placed,
        out_specs=(P(None, ROW, COL, None), P(None, ROW, COL, None)),
        check_vma=False,
    )
```

```python
import functools
import math

import jax
import jax.numpy as jnp
from jax import lax
from jax.experimental import pallas as pl
from jax.experimental.pallas import tpu as pltpu
from jax.sharding import Mesh
from jax.sharding import PartitionSpec as P

HDIM = 128
LAT = 16
PATCH = 2
KEYS = 128
NEG = -1e30


BF = jnp.bfloat16
F32 = jnp.float32


def full_call(body, out_shape, scratch=(), limit=24 * 1024 * 1024, **specs):
    return pl.pallas_call(
        body,
        out_shape=out_shape,
        scratch_shapes=list(scratch),
        compiler_params=pltpu.CompilerParams(vmem_limit_bytes=limit),
        **specs,
    )


def two_parts(value):
    high = value.astype(BF).astype(F32)
    low = (value - high).astype(BF).astype(F32)
    return high, low


def block_body(age_ref, history_ref, cache_k_ref, span_k_ref, cache_v_ref, span_v_ref, out_ref):
    slots, width = cache_k_ref.shape
    tokens = span_k_ref.shape[0]
    live = slots + tokens
    out_ref[0:slots] = cache_k_ref[...]
    out_ref[slots:live] = span_k_ref[...]
    out_ref[KEYS : KEYS + slots] = cache_v_ref[...]
    out_ref[KEYS + slots : KEYS + live] = span_v_ref[...]
    out_ref[KEYS + live :] = jnp.zeros((KEYS - live, width), BF)
    valid = jnp.where(age_ref[...] < history_ref[...], 1.0, 0.0)
    flags = jnp.concatenate(
        [valid, jnp.ones((1, tokens), F32), jnp.zeros((1, width - live), F32)], axis=1
    )
    out_ref[live:KEYS] = jnp.broadcast_to(flags, (KEYS - live, width)).astype(BF)


def attend_body(q_ref, near_ref, far_ref, out_ref, *, heads, tokens, step):
    places = q_ref.shape[0]
    groups = tokens // 8
    rate = math.log2(math.e) / math.sqrt(HDIM)
    rows = step * tokens
    row = lax.broadcasted_iota(jnp.int32, (rows, 128), 0)
    lane = lax.broadcasted_iota(jnp.int32, (rows, 128), 1)
    group_lane = lane - heads * ((row % tokens) // 8)
    lane_key = lax.broadcasted_iota(jnp.int32, (2 * KEYS, HDIM), 1)
    value_tail = jnp.where(lane_key == 0, 1.0, 0.0).astype(BF)
    masks = []
    for ref in (near_ref, far_ref):
        flags = [ref[d, KEYS - 8 : KEYS, 0:KEYS].astype(F32)[0:1] for d in range(2)]
        masks.append((1.0 - jnp.concatenate(flags, axis=1)) * NEG)
    for head in range(heads):
        cols = slice(head * HDIM, (head + 1) * HDIM)
        keys = [ref[:, 0:KEYS, cols].reshape(2 * KEYS, HDIM) for ref in (near_ref, far_ref)]
        vals = [
            jnp.concatenate([ref[:, KEYS : 2 * KEYS, cols].reshape(2 * KEYS, HDIM), value_tail], axis=1)
            for ref in (near_ref, far_ref)
        ]
        for start in range(0, places, step):
            query = q_ref[start : start + step, :, cols].reshape(rows, HDIM)
            scores = [
                lax.dot_general(query, k, (((1,), (1,)), ((), ())), preferred_element_type=F32) + mask
                for k, mask in zip(keys, masks)
            ]
            top = jnp.max(jnp.maximum(scores[0], scores[1]), axis=1, keepdims=True)
            top_high, top_low = two_parts(top)
            top = top_high + top_low
            out = sum(
                jnp.dot(jnp.exp2((s - top) * rate).astype(BF), v, preferred_element_type=F32)
                for s, v in zip(scores, vals)
            )
            sum_high, sum_low = two_parts(out[:, HDIM : HDIM + 1])
            at = slice(head * tokens, (head + 1) * tokens)
            out_ref[start : start + step, at, :] = out[:, 0:HDIM].reshape(step, tokens, HDIM).astype(BF)
            stats = jnp.zeros((rows, 128), F32)
            for k, part in enumerate((top_high, top_low, sum_high, sum_low)):
                stats = jnp.where(group_lane == 32 * k + head, part, stats)
            folded = stats.reshape(step, groups, 8, 128).sum(axis=1)
            at = slice(heads * tokens, heads * tokens + 8)
            if head:
                folded = folded + out_ref[start : start + step, at, :].astype(F32)
            out_ref[start : start + step, at, :] = folded.astype(BF)


def merge_body(in_ref, out_ref, *, heads, tokens):
    groups = tokens // 8
    stats = in_ref[:, heads * tokens :, :].astype(F32)
    top = stats + pltpu.roll(stats, 96, 2)
    total = pltpu.roll(stats, 64, 2) + pltpu.roll(stats, 32, 2)
    peak = jnp.max(top, axis=0, keepdims=True)
    factor = jnp.exp((top - peak) * (1.0 / math.sqrt(HDIM)))
    lane = lax.broadcasted_iota(jnp.int32, (1, 8, 128), 2)
    total = jnp.where(lane < groups * heads, total, 1.0)
    factor = jnp.where(lane < groups * heads, factor, 1.0)
    share = factor / jnp.sum(factor * total, axis=0, keepdims=True)
    for head in range(heads):
        for group in range(groups):
            at = head * tokens + group * 8
            weight = share[:, :, group * heads + head : group * heads + head + 1]
            part = in_ref[:, at : at + 8, :].astype(F32) * weight
            out_ref[group * 8 : group * 8 + 8, head * HDIM : (head + 1) * HDIM] = jnp.sum(
                part, axis=0
            ).astype(BF)


def project_body(att_ref, weight_ref, out_ref, rows_ref, *, frames, token_rows):
    count = att_ref.shape[0]
    tokens = frames * token_rows
    chunks, rows, _ = out_ref.shape
    i = lax.broadcasted_iota(jnp.int32, (count, count), 0)
    j = lax.broadcasted_iota(jnp.int32, (count, count), 1)
    chunk = i % chunks
    source = (chunk // token_rows) * tokens + (i // chunks) * token_rows + chunk % token_rows
    order = jnp.where(j == source, 1.0, 0.0).astype(BF)
    att = jnp.dot(order, att_ref[...], preferred_element_type=F32).astype(BF)
    out = lax.dot_general(att, weight_ref[...], (((1,), (1,)), ((), ())), preferred_element_type=F32)
    blocks = out.shape[1] // 128
    for block in range(blocks):
        for frame in range(frames):
            rows_ref[pl.ds(block * frames + frame, chunks, stride=rows), :] = out[
                frame * chunks : (frame + 1) * chunks, block * 128 : (block + 1) * 128
            ]
    for row in range(blocks * frames, rows):
        rows_ref[pl.ds(row, chunks, stride=rows), :] = jnp.zeros((chunks, 128), F32)
    out_ref[...] = rows_ref[...].reshape(chunks, rows, 128).astype(BF)


def head_body(
    in_ref, stream_ref, gate_ref, shift_ref, scale_ref, weight_ref, cache_ref, stream_out_ref, cells_ref, sum_ref, *, blocks
):
    parts = in_ref.shape[0] // blocks
    frames, features = stream_ref.shape
    size = features // blocks
    for block in range(blocks):
        total = in_ref[block * parts].astype(F32)
        for k in range(1, parts):
            total = total + in_ref[block * parts + k].astype(F32)
        total = jnp.concatenate([total[k * frames : (k + 1) * frames] for k in range(size // 128)], axis=1)
        sum_ref[:, block * size : (block + 1) * size] = total
    mixed = (stream_ref[...].astype(F32) + gate_ref[...] * sum_ref[...]).astype(BF)
    stream_out_ref[...] = mixed
    mixed = mixed.astype(F32)
    mean = jnp.mean(mixed, axis=-1, keepdims=True)
    centred = mixed - mean
    variance = jnp.mean(centred * centred, axis=-1, keepdims=True)
    normed = (centred * lax.rsqrt(variance + 1e-06) * (1.0 + scale_ref[...]) + shift_ref[...]).astype(BF)
    patch = lax.dot_general(
        normed, weight_ref[...], (((1,), (1,)), ((), ())), preferred_element_type=F32
    ).astype(BF)
    peers, rows, lanes = cells_ref.shape
    cells = jnp.concatenate([cache_ref[...].astype(F32), patch.astype(F32)], axis=0)
    cells = jnp.concatenate([cells, jnp.zeros((rows - cells.shape[0], cells.shape[1]), F32)], axis=0)
    cells = jnp.concatenate([cells, jnp.zeros((rows, lanes - cells.shape[1]), F32)], axis=1)
    cells_ref[...] = jnp.broadcast_to(cells[None], cells_ref.shape).astype(BF)


def conv_body(in_ref, weight_ref, gain_ref, out_ref, patch_ref, *, frames, token_rows, cols):
    core = lax.axis_index("core")
    col = lax.axis_index("xl") * (cols // 2) + lax.axis_index("z") * 2 + core
    row = lax.axis_index("y") * 2 + lax.axis_index("xh")
    inner = (col > 0) & (col < cols - 1)

    def cells(at_core, place, at_row, exists):
        found = in_ref[at_core, place * token_rows + jnp.clip(at_row, 0, token_rows - 1)].astype(F32)
        return jnp.where((at_row >= 0) & (at_row < token_rows) & exists, found, 0.0)

    by_col = [[], [], []]
    for step in (-1, 0, 1):
        beside = cells(1 - core, core, row + step, True)
        across = cells(core, core, row + step, inner)
        by_col[0].append(jnp.where(core == 1, beside, across))
        by_col[1].append(cells(core, 1 - core, row + step, True))
        by_col[2].append(jnp.where(core == 1, across, beside))
    for a in range(PATCH):
        for b in range(PATCH):
            pieces = []
            for u in range(3):
                for v in range(3):
                    for w in range(3):
                        i, j = a + v - 1, b + w - 1
                        block = by_col[j // 2 + 1][i // 2 + 1]
                        at = ((i % 2) * 2 + (j % 2)) * LAT
                        pieces.append(block[u : u + frames, at : at + LAT])
            patch_ref[(a * 2 + b) * 8 : (a * 2 + b) * 8 + frames, :] = jnp.concatenate(pieces, axis=1)
    patches = patch_ref[...].astype(BF)
    conv = jnp.dot(patches, weight_ref[...], preferred_element_type=F32)
    square = jnp.mean(conv * conv, axis=-1, keepdims=True)
    scaled = conv * lax.rsqrt(square + 1e-06) * gain_ref[...]
    silu = (scaled / (1.0 + jnp.exp(-scaled))).astype(BF)
    for f in range(frames):
        for a in range(PATCH):
            for b in range(PATCH):
                at = (a * 2 + b) * 8 + f
                out_ref[f, a, b : b + 1, :] = silu[at : at + 1, :]


COL = ("xl", "z", "core")
ROW = ("y", "xh")


def local(
    stream,
    queries,
    span_k,
    span_v,
    cache_k,
    cache_v,
    cache_age,
    history,
    out_weight,
    attn_gate,
    head_shift,
    head_scale,
    head_weight,
    latent_cache,
    conv_weight,
    rms_gain,
):
    frames, token_rows, _, width = queries.shape
    tokens = frames * token_rows
    heads = width // HDIM
    places = lax.axis_size("z")
    features = stream.shape[-1]

    weights = lax.all_gather(out_weight.T, ("z", "core"), axis=0, tiled=True)

    own = full_call(
        block_body,
        jax.ShapeDtypeStruct((2 * KEYS, width), BF),
        limit=None,
    )(
        cache_age[None, :],
        history[None, :],
        cache_k,
        span_k.reshape(tokens, width),
        cache_v,
        span_v.reshape(tokens, width),
    )
    near = lax.all_gather(own, "core", axis=0)
    far = lax.ppermute(near, "xl", [(0, 1), (1, 0)])
    gathered = lax.all_gather(queries.reshape(tokens, width), "z", axis=0)
    partial = full_call(
        functools.partial(attend_body, heads=heads, tokens=tokens, step=8),
        jax.ShapeDtypeStruct((places, heads * tokens + 8, HDIM), BF),
    )(gathered, near, far)
    partial = lax.all_to_all(partial, "z", 0, 0, tiled=True)
    attended = full_call(
        functools.partial(merge_body, heads=heads, tokens=tokens),
        jax.ShapeDtypeStruct((tokens, width), BF),
    )(partial)
    group = lax.all_gather(attended, "xl", axis=0, tiled=True)
    terms = full_call(
        functools.partial(project_body, frames=frames, token_rows=token_rows),
        jax.ShapeDtypeStruct((2 * token_rows, 64, 128), BF),
        [pltpu.VMEM((2 * token_rows * 64, 128), F32)],
    )(group, weights)
    terms = lax.all_to_all(terms, ("xl",) + ROW, 0, 0, tiled=True)
    stream_out, cells = full_call(
        functools.partial(head_body, blocks=2),
        (
            jax.ShapeDtypeStruct((frames, features), BF),
            jax.ShapeDtypeStruct((2 * token_rows, 8, 128), BF),
        ),
        [pltpu.VMEM((frames, features), F32)],
    )(
        terms,
        stream.reshape(frames, features),
        attn_gate[None, :],
        head_shift[None, :],
        head_scale[None, :],
        head_weight.T,
        latent_cache.reshape(2, -1),
    )
    cols = 2 * lax.axis_size("xl") * places
    starts = [(k, k + 1) for k in range(1, cols - 1, 2)] + [(cols - 1, 0)]
    pairs = [[c * token_rows + r for c in pair for r in range(token_rows)] for pair in starts]
    cells = lax.all_to_all(cells, COL + ROW, 0, 0, tiled=True, axis_index_groups=pairs)
    cells = lax.all_gather(cells, "core", axis=0)
    decoded = full_call(
        functools.partial(conv_body, frames=frames, token_rows=token_rows, cols=cols),
        jax.ShapeDtypeStruct((frames, PATCH, PATCH, conv_weight.shape[1]), BF),
        [pltpu.VMEM((32, conv_weight.shape[0]), F32)],
    )(cells, conv_weight, rms_gain[None, :])
    return stream_out.reshape(stream.shape), decoded


def solution(mesh):
    fine = Mesh(mesh.devices.reshape(2, 16, 2, 4, 2), COL + ROW)
    placed = (
        P(None, ROW, COL, None),
        P(None, None, COL, ROW),
        P(None, None, COL, ROW),
        P(None, None, COL, ROW),
        P(COL, ROW),
        P(COL, ROW),
        P(COL),
        P(),
        P(ROW, COL),
        P(),
        P(),
        P(),
        P(),
        P(None, ROW, COL, None),
        P(),
        P(),
    )
    return jax.shard_map(
        local,
        mesh=fine,
        in_specs=placed,
        out_specs=(P(None, ROW, COL, None), P(None, ROW, COL, None)),
        check_vma=False,
    )
```
